32 devices in a mesh: dp: 4 (over y, x), tp: 8 (over z, core).
Axes of the slice: x: 2, y: 2, z: 4, core: 2. Of those that a mesh axis runs over, the one named last changes fastest.
Arguments:
- gate_pre: bfloat16 [1024, 28672], P('dp', 'tp'), may hold values from -9 to 9
- up_pre: bfloat16 [1024, 28672], P('dp', 'tp'), may hold values from -9 to 9
- token_live: int32 [1024], P('dp'), may hold values from 0 to 1, as said below
- slab_offset: int32 [8], replicated, may hold values from 0 to 2048
Outputs:
- slab_cov: float32 [28672, 12288], P('dp', 'tp')
The draws below stay inside these ranges and needn't reach their ends.
Inputs may be any that keep to these rules, and one draw needn't show every extreme that they name: `token_live`: the first token of each block of 256 tokens is live.
All inputs are finite; a program needn't handle non-finite values.
Results may differ from the reference program's by a relative error of at most 0.004.
Values may be sent and summed in bfloat16 or wider, within the bound.
No kernel may reach another device: no remote copies, remote signals or barrier semaphores. Data moves between devices by JAX's collectives and lax.ppermute only.
A program may use at most 192 MiB of HBM per device.

```python
import jax
import jax.numpy as jnp
from jax import lax

FF = 28672
TOK_DEV = 256
SLAB_DEV = 1536
TOKENS = 1024
N_TP = 8


def draw_token_live(key, part):
    position = jnp.arange(TOKENS, dtype=jnp.int32)
    block_id = position // TOK_DEV
    block_total = TOKENS // TOK_DEV
    threshold = 30 + 60 * block_id // max(block_total - 1, 1)
    dice = jax.random.randint(key, (TOKENS,), 0, 100, dtype=jnp.int32)
    live_mask = (dice < threshold) | (position % TOK_DEV == 0)
    return live_mask.astype(jnp.int32)


def touch_ends(entries, key, least, largest):
    longest = entries.shape.index(max(entries.shape))
    spots = []
    for shift in (0, 1):
        where = [jax.random.randint(jax.random.fold_in(key, axis), (), 0, length) for axis, length in enumerate(entries.shape)]
        where[longest] = (where[longest] + shift) % entries.shape[longest]
        spots.append(tuple(where))
    return entries.at[spots[0]].set(least).at[spots[1]].set(largest)


def block_levels(key, dims, cuts, low, high):
    level, own = 1.0, jax.random.fold_in(key, 6)
    for dim, parts in cuts:
        steps = jnp.exp(jax.random.uniform(jax.random.fold_in(own, dim), (parts,), jnp.float32, low / len(cuts), high / len(cuts)))
        level = level * jnp.repeat(steps, dims[dim] // parts).reshape([-1 if axis == dim else 1 for axis in range(len(dims))])
    return level


def centred(stream_key, shape, width, most, pieces=(), kind=jnp.bfloat16):
    drawn = width * jax.random.normal(stream_key, shape, jnp.float32)
    if pieces:
        drawn = drawn * block_levels(stream_key, shape, pieces, -0.22, 0.18)
    return jnp.clip(drawn, -most, most).astype(kind)


def setup_inputs(seed: int = 0) -> dict:
    key_list = jax.random.split(jax.random.key(seed), 5)
    gate_pre = centred(key_list[0], (TOKENS, FF), 1.5, 9.0, ((0, 4), (1, 8)))
    up_pre = centred(key_list[1], (TOKENS, FF), 1.5, 9.0, ((0, 4), (1, 8)))
    token_live = draw_token_live(jax.random.fold_in(key_list[4], 71), 0)
    slab_offset = touch_ends(jax.random.randint(key_list[3], (N_TP,), 0, FF // N_TP - SLAB_DEV + 1), jax.random.fold_in(key_list[3], 1), 0, (FF // N_TP - SLAB_DEV + 1) - 1).astype(jnp.int32)
    return {"gate_pre": gate_pre, "up_pre": up_pre, "token_live": token_live, "slab_offset": slab_offset}


def reference(gate_pre, up_pre, token_live, slab_offset):
    live_mask = token_live.astype(jnp.float32)
    keys_all = (jax.nn.silu(gate_pre.astype(jnp.float32)) * up_pre.astype(jnp.float32) * live_mask[:, None]).astype(jnp.bfloat16)
    live_total = jnp.sum(live_mask)
    shard_width = FF // N_TP
    starts = jnp.arange(N_TP, dtype=jnp.int32) * shard_width + slab_offset.astype(jnp.int32)
    columns = (starts[:, None] + jnp.arange(SLAB_DEV, dtype=jnp.int32)[None, :]).reshape(N_TP * SLAB_DEV)
    slab_cols = jnp.take(keys_all, columns, axis=1)
    gram_all = lax.dot_general(keys_all, slab_cols, (((0,), (0,)), ((), ())), preferred_element_type=jnp.float32)
    return gram_all / live_total
```

```python
import functools

import jax
import jax.numpy as jnp
from jax import lax
from jax.experimental import pallas as pl
from jax.experimental.pallas import tpu as pltpu
from jax.sharding import PartitionSpec as P

SLAB_DEV = 1536
UNIT = 256
SLOTS = 4


def keys_kernel(room, cuts, live_ref, gate_ref, up_ref, *refs):
    own_refs, spare_refs, order_ref = refs[: len(cuts) - 1], refs[len(cuts) - 1 : -1], refs[-1]
    tokens = gate_ref.shape[0]
    step = pl.program_id(0)

    @pl.when(step == 0)
    def _():
        live = live_ref[...].astype(jnp.float32)
        slot_id = lax.broadcasted_iota(jnp.int32, (tokens, tokens), 0)
        token_id = lax.broadcasted_iota(jnp.int32, (tokens, tokens), 1)
        upto = (slot_id <= token_id).astype(jnp.float32)
        rank = (jnp.dot(jnp.broadcast_to(live, (8, tokens)), upto, preferred_element_type=jnp.float32) - 1.0)[:1]
        total = jnp.sum(live)
        slot = jnp.where(rank < room, rank, tokens - total + rank)
        taken = (slot_id.astype(jnp.float32) == slot) & (live > 0)
        order_ref[...] = taken.astype(jnp.bfloat16)

    gate = gate_ref[...].astype(jnp.float32)
    key = gate / (1.0 + jnp.exp(-gate)) * up_ref[...].astype(jnp.float32)
    placed = jnp.dot(
        order_ref[...], key.astype(jnp.bfloat16), preferred_element_type=jnp.float32
    ).astype(jnp.bfloat16)
    for c in range(len(cuts) - 1):

        @pl.when((step >= cuts[c]) & (step < cuts[c + 1]))
        def _(c=c):
            own_refs[c][...] = placed[:room]

    @pl.when(step < cuts[1])
    def _():
        spare_refs[0][...] = placed[room:]

    @pl.when(step >= cuts[1])
    def _():
        spare_refs[1][...] = placed[room:]


def live_keys(gate_pre, up_pre, token_live, room, widths):
    tokens, width = gate_pre.shape
    spare = tokens - room
    cuts = [sum(widths[:i]) // UNIT for i in range(len(widths) + 1)]
    spans = [(cuts[i], cuts[i + 1]) for i in range(len(widths))]
    spare_spans = [(0, cuts[1]), (cuts[1], cuts[-1])]

    def spec(height, span):
        low, high = span
        return pl.BlockSpec((height, UNIT), lambda i: (0, jnp.clip(i - low, 0, high - low - 1)))

    def shape(height, span):
        return jax.ShapeDtypeStruct((height, (span[1] - span[0]) * UNIT), jnp.bfloat16)

    outs = pl.pallas_call(
        functools.partial(keys_kernel, room, cuts),
        grid=(width // UNIT,),
        in_specs=[
            pl.BlockSpec((1, tokens), lambda i: (0, 0)),
            pl.BlockSpec((tokens, UNIT), lambda i: (0, i)),
            pl.BlockSpec((tokens, UNIT), lambda i: (0, i)),
        ],
        out_specs=[spec(room, span) for span in spans] + [spec(spare, span) for span in spare_spans],
        out_shape=[shape(room, span) for span in spans] + [shape(spare, span) for span in spare_spans],
        scratch_shapes=[pltpu.VMEM((tokens, tokens), jnp.bfloat16)],
        cost_estimate=pl.CostEstimate(
            flops=2 * tokens * tokens * width,
            bytes_accessed=6 * tokens * width,
            transcendentals=tokens * width,
        ),
        name="live_keys",
    )(token_live[None, :], gate_pre, up_pre)
    return outs[: len(widths)], outs[len(widths) :]


def gram_kernel(rows_ref, inv_ref, *refs):
    out_ref, held, sent = refs[-3:]
    slab_ref = refs[0]
    lefts = refs[1 : 1 + rows_ref.shape[0]]
    slots = held.shape[0]
    tiles = lefts[0].shape[1] // UNIT

    def leave(row, slot):
        row = pl.multiple_of(row, UNIT)
        return pltpu.make_async_copy(held.at[slot], out_ref.at[pl.ds(row, UNIT)], sent.at[slot])

    for side, left_ref in enumerate(lefts):

        def tile(i, carry, side=side, left_ref=left_ref):
            slot = lax.rem(i + side * tiles, slots)

            @pl.when(i + side * tiles >= slots)
            def _():
                leave(0, slot).wait()

            left = left_ref[:, pl.ds(pl.multiple_of(i * UNIT, UNIT), UNIT)]
            gram = lax.dot_general(
                left, slab_ref[...], (((0,), (0,)), ((), ())), preferred_element_type=jnp.float32
            )
            held[slot] = gram * inv_ref[0]
            leave(rows_ref[side] + i * UNIT, slot).start()
            return carry

        lax.fori_loop(0, tiles, tile, 0)
    for slot in range(slots):
        leave(0, slot).wait()


def gram_rows(lefts, starts, slab, inv, out, rows):
    depth, width = lefts[0].shape
    cols = slab.shape[1]
    in_specs = [pl.BlockSpec(memory_space=pltpu.SMEM)] * 2
    in_specs += [pl.BlockSpec(memory_space=pltpu.VMEM)] * (1 + len(lefts))
    operands = [jnp.stack(starts), inv, slab, *lefts]
    aliases = {}
    if out is not None:
        in_specs += [pl.BlockSpec(memory_space=pl.ANY)]
        aliases = {len(operands): 0}
        operands.append(out)
    slots = min(SLOTS, len(lefts) * width // UNIT)
    return pl.pallas_call(
        gram_kernel,
        in_specs=in_specs,
        out_specs=pl.BlockSpec(memory_space=pl.ANY),
        out_shape=jax.ShapeDtypeStruct((rows, cols), jnp.float32),
        scratch_shapes=[pltpu.VMEM((slots, UNIT, cols), jnp.float32), pltpu.SemaphoreType.DMA((slots,))],
        input_output_aliases=aliases,
        compiler_params=pltpu.CompilerParams(vmem_limit_bytes=20 << 20),
        cost_estimate=pl.CostEstimate(
            flops=2 * len(lefts) * depth * width * cols,
            bytes_accessed=4 * len(lefts) * width * cols,
            transcendentals=0,
        ),
        name="gram_rows",
    )(*operands)


def chunk_widths(width):
    units = width // UNIT
    shares = (3, 5, 4, 2)
    cuts = [units * sum(shares[:i]) // sum(shares) for i in range(len(shares) + 1)]
    return [UNIT * (cuts[i + 1] - cuts[i]) for i in range(len(shares)) if cuts[i + 1] > cuts[i]]


def pick(which, values):
    result = values[0]
    for index in range(1, len(values)):
        result = jnp.where(which == index, values[index], result)
    return result


def tied(value, *after):
    return lax.optimization_barrier((value, *after))[0]


def exchange(n_dp, n_tp, chunks, slab_here, inv):
    line = n_tp // 2
    me_dp, me_tp = lax.axis_index("dp"), lax.axis_index("tp")
    me_line, core = me_tp // 2, me_tp % 2
    count = len(chunks)
    starts = [sum(chunk.shape[1] for chunk in chunks[:i]) for i in range(count)]
    half = starts[-1] + chunks[-1].shape[1]
    rows = 2 * half * line // n_dp
    chunks = list(chunks)

    def swap_dp(value, j):
        return lax.ppermute(value, "dp", [(s, s ^ j) for s in range(n_dp)])

    def swap_core(value):
        return lax.ppermute(value, "tp", [(s, s ^ 1) for s in range(n_tp)])

    def move_line(value, target):
        return lax.ppermute(
            value, "tp", [(2 * s + c, 2 * target(s) + c) for s in range(line) for c in range(2)]
        )

    def tie(value, *stages):
        after = [part for stage in stages if stage is not None for part in stage]
        return tied(value, *after) if after else value

    direct = line // 2 + 1 if line == 4 else line
    near, held, crossed, mine, other = ({} for _ in range(5))
    out, slab = None, None
    for slot in range(count + 4):
        i = slot - 1
        if 0 <= i < count:
            held[i] = list(near[i])
            if direct < line:
                relay = jnp.where((me_line == 0) | (me_line == 3), near[i][1], near[i][2])
                held[i].append(move_line(relay, lambda s: (2, 0, 3, 1)[s]))
        i = slot
        if i < count:
            own = tie(chunks[i], near.get(i - 1), crossed.get(i - 3))
            near[i] = [own] + [move_line(own, lambda s, k=k: s ^ k) for k in range(1, direct)]
        if slot == 0:
            slabs = [slab_here] + [swap_dp(slab_here, j) for j in range(1, n_dp)]
        if slot == 1:
            slab = jnp.concatenate(slabs, axis=0)
        i = slot - 2
        if 0 <= i < count:
            picked = [pick(me_line ^ me_dp ^ j, held[i]) for j in range(n_dp)]
            if out is not None:
                picked[0], out = lax.optimization_barrier((picked[0], out))
            crossed[i] = [picked[0]] + [swap_dp(picked[j], j) for j in range(1, n_dp)]
        i = slot - 3
        if 0 <= i < count:
            mine[i] = jnp.concatenate(crossed[i], axis=0)
            other[i] = swap_core(mine[i])
        if 0 <= i < count:
            base = [side * half + starts[i] for side in (core, 1 - core)]
            if i < count - 1:
                out = gram_rows([mine[i], other[i]], base, slab, inv, out, rows)
            else:
                out = gram_rows([mine[i]], base[:1], slab, inv, out, rows)
                out = gram_rows([other[i]], base[1:], slab, inv, out, rows)
    return out


def share_rows(n_dp, n_tp, room, owns, spares, slab_offset, inv):
    kept = room - spares[0].shape[0]

    def mirror(value):
        return lax.ppermute(value, "dp", [(s, n_dp - 1 - s) for s in range(n_dp)])

    first = mirror(spares[0])
    rest = mirror(tied(spares[1], first))
    chunks, start = [], 0
    for own in owns:
        width = own.shape[1]
        extra = rest[:, start : start + width] if chunks else first
        start += width if chunks else 0
        chunks.append(jnp.concatenate([own[:kept], own[kept:] + extra], axis=0))
    slab_here = lax.dynamic_slice_in_dim(
        jnp.concatenate(chunks, axis=1), slab_offset[lax.axis_index("tp")], SLAB_DEV, 1
    )
    return exchange(n_dp, n_tp, chunks, slab_here, inv)


def all_rows(n_dp, n_tp, owns, spares, slab_offset, inv):
    chunks, start = [], 0
    for own in owns:
        width = own.shape[1]
        extra = spares[1][:, start : start + width] if chunks else spares[0]
        start += width if chunks else 0
        chunks.append(jnp.concatenate([own, extra], axis=0))
    slab_here = lax.dynamic_slice_in_dim(
        jnp.concatenate(chunks, axis=1), slab_offset[lax.axis_index("tp")], SLAB_DEV, 1
    )
    return exchange(n_dp, n_tp, chunks, slab_here, inv)


def on_device(n_dp, n_tp, gate_pre, up_pre, token_live, slab_offset):
    tokens, half = gate_pre.shape
    room = tokens * 11 // 16
    masks = [token_live] + [
        lax.ppermute(token_live, "dp", [(s, s ^ j) for s in range(n_dp)]) for j in range(1, n_dp)
    ]
    owns, spares = live_keys(gate_pre, up_pre, token_live, room, chunk_widths(half))
    tallies = [jnp.sum(mask) for mask in masks]
    inv = (1.0 / sum(tallies).astype(jnp.float32)).reshape(1)
    fits = jnp.bool_(True)
    for j in range(n_dp):
        fits &= tallies[j] + tallies[n_dp - 1 - j] <= 2 * room
    return lax.cond(
        fits,
        functools.partial(share_rows, n_dp, n_tp, room),
        functools.partial(all_rows, n_dp, n_tp),
        owns, spares, slab_offset, inv,
    )


def solution(mesh):
    placed = (P("dp", "tp"), P("dp", "tp"), P("dp"), P())
    return jax.shard_map(
        functools.partial(on_device, mesh.shape["dp"], mesh.shape["tp"]),
        mesh=mesh,
        in_specs=placed,
        out_specs=P("dp", "tp"),
        check_vma=False,
    )
```

```python
import functools

import jax
import jax.numpy as jnp
from jax import lax
from jax.experimental import pallas as pl
from jax.experimental.pallas import tpu as pltpu
from jax.sharding import PartitionSpec as P

SLAB_DEV = 1536
UNIT = 256
SLOTS = 4
SHARES = (4, 4, 4, 2)


def keys_kernel(room, widths, live_ref, gate_ref, up_ref, *refs):
    own_refs, spare_refs = refs[: len(widths)], refs[len(widths) :]
    tokens = gate_ref.shape[0]
    live = live_ref[...].astype(jnp.float32)
    slot_id = lax.broadcasted_iota(jnp.int32, (tokens, tokens), 0)
    token_id = lax.broadcasted_iota(jnp.int32, (tokens, tokens), 1)
    upto = (slot_id <= token_id).astype(jnp.float32)
    rank = (jnp.dot(jnp.broadcast_to(live, (8, tokens)), upto, preferred_element_type=jnp.float32) - 1.0)[:1]
    slot = jnp.where(rank < room, rank, tokens - jnp.sum(live) + rank)
    order = ((slot_id.astype(jnp.float32) == slot) & (live > 0)).astype(jnp.bfloat16)

    def place(columns):
        gate = gate_ref[:, columns].astype(jnp.float32)
        key = (0.5 * gate) * (1.0 + jnp.tanh(0.5 * gate)) * up_ref[:, columns].astype(jnp.float32)
        return jnp.dot(order, key.astype(jnp.bfloat16), preferred_element_type=jnp.float32).astype(jnp.bfloat16)

    for c, width in enumerate(widths):
        start = sum(widths[:c])
        shift = start - widths[0] if c else 0

        def fill(i, carry, c=c, start=start, shift=shift):
            at = pl.multiple_of(i * UNIT, UNIT)
            placed = place(pl.ds(start + at, UNIT))
            own_refs[c][:, pl.ds(at, UNIT)] = placed[:room]
            spare_refs[min(c, 1)][:, pl.ds(shift + at, UNIT)] = placed[room:]
            return carry

        lax.fori_loop(0, width // UNIT, fill, 0)


def live_keys(gate_pre, up_pre, token_live, room, widths):
    tokens, width = gate_pre.shape
    spare = tokens - room
    shapes = [(room, part) for part in widths] + [(spare, widths[0]), (spare, width - widths[0])]
    outs = pl.pallas_call(
        functools.partial(keys_kernel, room, widths),
        in_specs=[pl.BlockSpec(memory_space=pltpu.VMEM)] * 3,
        out_specs=[pl.BlockSpec(memory_space=pltpu.VMEM)] * len(shapes),
        out_shape=[jax.ShapeDtypeStruct(shape, jnp.bfloat16) for shape in shapes],
        compiler_params=pltpu.CompilerParams(vmem_limit_bytes=12 << 20),
        cost_estimate=pl.CostEstimate(
            flops=2 * tokens * tokens * width,
            bytes_accessed=6 * tokens * width,
            transcendentals=tokens * width,
        ),
        name="live_keys",
    )(token_live, gate_pre, up_pre)
    return outs[: len(widths)], outs[len(widths) :]


def join_kernel(*refs):
    parts, out_ref = refs[:-1], refs[-1]
    rows = parts[0].shape[0]
    for i, part in enumerate(parts):
        out_ref[i * rows : (i + 1) * rows, :] = part[...]


def joined(parts):
    rows, cols = parts[0].shape
    return pl.pallas_call(
        join_kernel,
        in_specs=[pl.BlockSpec(memory_space=pltpu.VMEM)] * len(parts),
        out_specs=pl.BlockSpec(memory_space=pltpu.VMEM),
        out_shape=jax.ShapeDtypeStruct((len(parts) * rows, cols), parts[0].dtype),
        compiler_params=pltpu.CompilerParams(vmem_limit_bytes=8 << 20),
        cost_estimate=pl.CostEstimate(flops=0, bytes_accessed=1 << 20, transcendentals=0),
        name="joined",
    )(*parts)


def deal_kernel(which_ref, *refs):
    count = len(refs) // 2
    for which in range(count):

        @pl.when(which_ref[0] == which)
        def _(which=which):
            for j in range(count):
                refs[count + j][...] = refs[j ^ which][...]


def dealt(which, values):
    return pl.pallas_call(
        deal_kernel,
        in_specs=[pl.BlockSpec(memory_space=pltpu.SMEM)] + [pl.BlockSpec(memory_space=pltpu.VMEM)] * len(values),
        out_specs=[pl.BlockSpec(memory_space=pltpu.VMEM)] * len(values),
        out_shape=[jax.ShapeDtypeStruct(value.shape, value.dtype) for value in values],
        compiler_params=pltpu.CompilerParams(vmem_limit_bytes=8 << 20),
        cost_estimate=pl.CostEstimate(flops=0, bytes_accessed=1 << 20, transcendentals=0),
        name="dealt",
    )(which, *values)


def gram_kernel(rows_ref, total_ref, *refs):
    out_ref, held, sent = refs[-3:]
    slab_ref = refs[0]
    lefts = refs[1 : 1 + rows_ref.shape[0]]
    slots = held.shape[0]
    tiles = lefts[0].shape[1] // UNIT
    inv = 1.0 / jnp.full((1, held.shape[2]), total_ref[0], jnp.float32)

    def leave(row, slot):
        row = pl.multiple_of(row, UNIT)
        return pltpu.make_async_copy(held.at[slot], out_ref.at[pl.ds(row, UNIT)], sent.at[slot])

    for side, left_ref in enumerate(lefts):

        def tile(i, carry, side=side, left_ref=left_ref):
            slot = lax.rem(i + side * tiles, slots)

            @pl.when(i + side * tiles >= slots)
            def _():
                leave(0, slot).wait()

            left = left_ref[:, pl.ds(pl.multiple_of(i * UNIT, UNIT), UNIT)]
            gram = lax.dot_general(
                left, slab_ref[...], (((0,), (0,)), ((), ())), preferred_element_type=jnp.float32
            )
            held[slot] = gram * inv
            leave(rows_ref[side] + i * UNIT, slot).start()
            return carry

        lax.fori_loop(0, tiles, tile, 0)
    for slot in range(slots):
        leave(0, slot).wait()


def gram_rows(lefts, starts, slab, total, out, rows):
    depth, width = lefts[0].shape
    cols = slab.shape[1]
    in_specs = [pl.BlockSpec(memory_space=pltpu.SMEM)] * 2
    in_specs += [pl.BlockSpec(memory_space=pltpu.VMEM)] * (1 + len(lefts))
    operands = [jnp.stack(starts), total, slab, *lefts]
    aliases = {}
    if out is not None:
        in_specs += [pl.BlockSpec(memory_space=pl.ANY)]
        aliases = {len(operands): 0}
        operands.append(out)
    slots = min(SLOTS, len(lefts) * width // UNIT)
    return pl.pallas_call(
        gram_kernel,
        in_specs=in_specs,
        out_specs=pl.BlockSpec(memory_space=pl.ANY),
        out_shape=jax.ShapeDtypeStruct((rows, cols), jnp.float32),
        scratch_shapes=[pltpu.VMEM((slots, UNIT, cols), jnp.float32), pltpu.SemaphoreType.DMA((slots,))],
        input_output_aliases=aliases,
        compiler_params=pltpu.CompilerParams(vmem_limit_bytes=20 << 20),
        cost_estimate=pl.CostEstimate(
            flops=2 * len(lefts) * depth * width * cols,
            bytes_accessed=4 * len(lefts) * width * cols,
            transcendentals=0,
        ),
        name="gram_rows",
    )(*operands)


def chunk_widths(width):
    units = width // UNIT
    shares = SHARES
    cuts = [units * sum(shares[:i]) // sum(shares) for i in range(len(shares) + 1)]
    return [UNIT * (cuts[i + 1] - cuts[i]) for i in range(len(shares)) if cuts[i + 1] > cuts[i]]


def tally_kernel(room, *refs):
    masks, total_ref, fits_ref = refs[:-2], refs[-2], refs[-1]
    tallies = [jnp.sum(ref[...].astype(jnp.float32)) for ref in masks]
    total_ref[0] = sum(tallies)
    fits = tallies[0] + tallies[-1] <= 2.0 * room
    for j in range(1, len(masks) // 2):
        fits &= tallies[j] + tallies[len(masks) - 1 - j] <= 2.0 * room
    fits_ref[0] = fits.astype(jnp.int32)


def tally(masks, room):
    return pl.pallas_call(
        functools.partial(tally_kernel, room),
        in_specs=[pl.BlockSpec(memory_space=pltpu.VMEM)] * len(masks),
        out_specs=[pl.BlockSpec(memory_space=pltpu.SMEM)] * 2,
        out_shape=[jax.ShapeDtypeStruct((1,), jnp.float32), jax.ShapeDtypeStruct((1,), jnp.int32)],
        name="tally",
    )(*masks)


def tied(value, *after):
    return lax.optimization_barrier((value, *after))[0]


def exchange(n_dp, n_tp, widths, first_chunk, later, slab_offset, total):
    line = n_tp // 2
    me_dp, me_tp = lax.axis_index("dp"), lax.axis_index("tp")
    me_line, core = me_tp // 2, me_tp % 2
    count = len(widths)
    starts = [sum(widths[:i]) for i in range(count)]
    half = sum(widths)
    rows = 2 * half * line // n_dp

    def swap_dp(value, j):
        return lax.ppermute(value, "dp", [(s, s ^ j) for s in range(n_dp)])

    def swap_core(value):
        return lax.ppermute(value, "tp", [(s, s ^ 1) for s in range(n_tp)])

    def move_line(value, target):
        return lax.ppermute(
            value, "tp", [(2 * s + c, 2 * target(s) + c) for s in range(line) for c in range(2)]
        )

    direct = line // 2 + 1 if line == 4 else line

    def spread(own):
        return [own] + [move_line(own, lambda s, k=k: s ^ k) for k in range(1, direct)]

    def grams(i, sides, mine, other, out):
        lefts = [(mine, other)[side] for side in sides]
        places = [(core, 1 - core)[side] * half + starts[i] for side in sides]
        return gram_rows(lefts, places, slab, total, out, rows)

    which = (me_line ^ me_dp).astype(jnp.int32).reshape(1)
    near = {0: spread(first_chunk)}
    late, merge = later()
    held, crossed = {}, {}
    chunks, out, slab, slabs = {}, None, None, None
    for slot in range(1, count + 3):
        near, held, crossed, chunks, late, slabs, out = lax.optimization_barrier(
            (near, held, crossed, chunks, late, slabs, out)
        )
        done, after = {}, {}
        i = slot - 1
        if i < count:
            after[i] = near.pop(i)
            if direct < line:
                relay = jnp.where((me_line == 0) | (me_line == 3), after[i][1], after[i][2])
                after[i] = after[i] + [move_line(relay, lambda s: (2, 0, 3, 1)[s])]
        if slot == 1:
            chunks = merge(late)
            late = None
        if slot < count:
            near[slot] = spread(chunks[slot])
        if slot == 1:
            slab_here = lax.dynamic_slice_in_dim(
                jnp.concatenate([first_chunk] + [chunks[c] for c in range(1, count)], axis=1),
                slab_offset[me_tp], SLAB_DEV, 1,
            )
            slabs = [slab_here] + [swap_dp(slab_here, j) for j in range(1, n_dp)]
        if slot == 2:
            slab = joined(slabs)
            slabs = None
        i = slot - 2
        if 0 <= i < count:
            picked = dealt(which, held.pop(i))
            done[i] = [picked[0]] + [swap_dp(picked[j], j) for j in range(1, n_dp)]
        i = slot - 3
        if 0 <= i < count:
            mine = joined(crossed.pop(i))
            other = swap_core(mine)
            if i + 1 < count:
                out = grams(i, (0, 1), mine, other, out)
            else:
                out = grams(i, (0,), mine, other, out)
                out = grams(i, (1,), mine, other, out)
        held.update(after)
        crossed.update(done)
    return out


def mirrored(n_dp, value):
    return lax.ppermute(value, "dp", [(s, n_dp - 1 - s) for s in range(n_dp)])


def share_rows(n_dp, n_tp, room, widths, owns, spares, first, slab_offset, total):
    kept = room - spares[0].shape[0]

    def merged(own, extra):
        return own + jnp.pad(extra, ((kept, 0), (0, 0)))

    def merge(rest):
        starts = [sum(widths[1:i]) for i in range(1, len(widths) + 1)]
        return {c: merged(owns[c], rest[:, starts[c - 1] : starts[c]]) for c in range(1, len(widths))}

    return exchange(
        n_dp, n_tp, widths, merged(owns[0], first), lambda: (mirrored(n_dp, spares[1]), merge), slab_offset, total
    )


def all_rows(n_dp, n_tp, widths, owns, spares, first, slab_offset, total):
    def merge(rest):
        starts = [sum(widths[1:i]) for i in range(1, len(widths) + 1)]
        return {
            c: jnp.concatenate([owns[c], rest[:, starts[c - 1] : starts[c]]], axis=0)
            for c in range(1, len(widths))
        }

    first_chunk = jnp.concatenate([owns[0], spares[0]], axis=0)
    return exchange(n_dp, n_tp, widths, first_chunk, lambda: (spares[1], merge), slab_offset, total)


def on_device(n_dp, n_tp, gate_pre, up_pre, token_live, slab_offset):
    tokens, half = gate_pre.shape
    room = tokens * 11 // 16
    widths = chunk_widths(half)
    live = token_live[None, :]
    masks = [live] + [lax.ppermute(live, "dp", [(s, s ^ j) for s in range(n_dp)]) for j in range(1, n_dp)]
    owns, spares = live_keys(gate_pre, up_pre, live, room, widths)
    first = mirrored(n_dp, spares[0])
    total, fits = tally(masks, room)
    return lax.cond(
        fits[0] > 0,
        functools.partial(share_rows, n_dp, n_tp, room, widths),
        functools.partial(all_rows, n_dp, n_tp, widths),
        owns, spares, first, slab_offset, total,
    )


def solution(mesh):
    placed = (P("dp", "tp"), P("dp", "tp"), P("dp"), P())
    return jax.shard_map(
        functools.partial(on_device, mesh.shape["dp"], mesh.shape["tp"]),
        mesh=mesh,
        in_specs=placed,
        out_specs=P("dp", "tp"),
        check_vma=False,
    )
```

```python
import functools

import jax
import jax.numpy as jnp
from jax import lax
from jax.experimental import pallas as pl
from jax.experimental.pallas import tpu as pltpu
from jax.sharding import PartitionSpec as P

SLAB_DEV = 1536
UNIT = 256
SLOTS = 4
SHARES = (4, 4, 4, 2)
FULL_SHARES = (7, 7)


def keys_kernel(room, widths, live_ref, gate_ref, up_ref, *refs):
    own_refs, spare_refs = refs[: len(widths)], refs[len(widths) :]
    tokens = gate_ref.shape[0]
    live = live_ref[...].astype(jnp.float32)
    slot_id = lax.broadcasted_iota(jnp.int32, (tokens, tokens), 0)
    token_id = lax.broadcasted_iota(jnp.int32, (tokens, tokens), 1)
    upto = (slot_id <= token_id).astype(jnp.float32)
    rank = (jnp.dot(jnp.broadcast_to(live, (8, tokens)), upto, preferred_element_type=jnp.float32) - 1.0)[:1]
    slot = jnp.where(rank < room, rank, tokens - jnp.sum(live) + rank)
    order = ((slot_id.astype(jnp.float32) == slot) & (live > 0)).astype(jnp.bfloat16)

    def place(columns):
        gate = gate_ref[:, columns].astype(jnp.float32)
        key = (0.5 * gate) * (1.0 + jnp.tanh(0.5 * gate)) * up_ref[:, columns].astype(jnp.float32)
        return jnp.dot(order, key.astype(jnp.bfloat16), preferred_element_type=jnp.float32).astype(jnp.bfloat16)

    for c, width in enumerate(widths):
        start = sum(widths[:c])
        shift = start - widths[0] if c else 0

        def fill(i, carry, c=c, start=start, shift=shift):
            at = pl.multiple_of(i * UNIT, UNIT)
            placed = place(pl.ds(start + at, UNIT))
            own_refs[c][:, pl.ds(at, UNIT)] = placed[:room]
            spare_refs[min(c, 1)][:, pl.ds(shift + at, UNIT)] = placed[room:]
            return carry

        lax.fori_loop(0, width // UNIT, fill, 0)


def live_keys(gate_pre, up_pre, token_live, room, widths):
    tokens, width = gate_pre.shape
    spare = tokens - room
    shapes = [(room, part) for part in widths] + [(spare, widths[0]), (spare, width - widths[0])]
    outs = pl.pallas_call(
        functools.partial(keys_kernel, room, widths),
        in_specs=[pl.BlockSpec(memory_space=pltpu.VMEM)] * 3,
        out_specs=[pl.BlockSpec(memory_space=pltpu.VMEM)] * len(shapes),
        out_shape=[jax.ShapeDtypeStruct(shape, jnp.bfloat16) for shape in shapes],
        compiler_params=pltpu.CompilerParams(vmem_limit_bytes=12 << 20),
        cost_estimate=pl.CostEstimate(
            flops=2 * tokens * tokens * width,
            bytes_accessed=6 * tokens * width,
            transcendentals=tokens * width,
        ),
        name="live_keys",
    )(token_live, gate_pre, up_pre)
    return outs[: len(widths)], outs[len(widths) :]


def join_kernel(*refs):
    parts, out_ref = refs[:-1], refs[-1]
    rows = parts[0].shape[0]
    for i, part in enumerate(parts):
        out_ref[i * rows : (i + 1) * rows, :] = part[...]


def joined(parts):
    rows, cols = parts[0].shape
    return pl.pallas_call(
        join_kernel,
        in_specs=[pl.BlockSpec(memory_space=pltpu.VMEM)] * len(parts),
        out_specs=pl.BlockSpec(memory_space=pltpu.VMEM),
        out_shape=jax.ShapeDtypeStruct((len(parts) * rows, cols), parts[0].dtype),
        compiler_params=pltpu.CompilerParams(vmem_limit_bytes=max(8 << 20, 10 * len(parts) * rows * cols)),
        cost_estimate=pl.CostEstimate(flops=0, bytes_accessed=1 << 20, transcendentals=0),
        name="joined",
    )(*parts)


def deal_kernel(which_ref, *refs):
    count = len(refs) // 2
    for which in range(count):

        @pl.when(which_ref[0] == which)
        def _(which=which):
            for j in range(count):
                refs[count + j][...] = refs[j ^ which][...]


def dealt(which, values):
    return pl.pallas_call(
        deal_kernel,
        in_specs=[pl.BlockSpec(memory_space=pltpu.SMEM)] + [pl.BlockSpec(memory_space=pltpu.VMEM)] * len(values),
        out_specs=[pl.BlockSpec(memory_space=pltpu.VMEM)] * len(values),
        out_shape=[jax.ShapeDtypeStruct(value.shape, value.dtype) for value in values],
        compiler_params=pltpu.CompilerParams(
            vmem_limit_bytes=max(8 << 20, 10 * len(values) * values[0].size)
        ),
        cost_estimate=pl.CostEstimate(flops=0, bytes_accessed=1 << 20, transcendentals=0),
        name="dealt",
    )(which, *values)


def gram_kernel(rows_ref, total_ref, *refs):
    out_ref, held, sent = refs[-3:]
    slab_ref = refs[0]
    lefts = refs[1 : 1 + rows_ref.shape[0]]
    slots = held.shape[0]
    tiles = lefts[0].shape[1] // UNIT
    inv = 1.0 / jnp.full((1, held.shape[2]), total_ref[0], jnp.float32)

    def leave(row, slot):
        row = pl.multiple_of(row, UNIT)
        return pltpu.make_async_copy(held.at[slot], out_ref.at[pl.ds(row, UNIT)], sent.at[slot])

    for side, left_ref in enumerate(lefts):

        def tile(i, carry, side=side, left_ref=left_ref):
            slot = lax.rem(i + side * tiles, slots)

            @pl.when(i + side * tiles >= slots)
            def _():
                leave(0, slot).wait()

            left = left_ref[:, pl.ds(pl.multiple_of(i * UNIT, UNIT), UNIT)]
            gram = lax.dot_general(
                left, slab_ref[...], (((0,), (0,)), ((), ())), preferred_element_type=jnp.float32
            )
            held[slot] = gram * inv
            leave(rows_ref[side] + i * UNIT, slot).start()
            return carry

        lax.fori_loop(0, tiles, tile, 0)
    for slot in range(slots):
        leave(0, slot).wait()


def gram_rows(lefts, starts, slab, total, out, rows):
    depth, width = lefts[0].shape
    cols = slab.shape[1]
    in_specs = [pl.BlockSpec(memory_space=pltpu.SMEM)] * 2
    in_specs += [pl.BlockSpec(memory_space=pltpu.VMEM)] * (1 + len(lefts))
    operands = [jnp.stack(starts), total, slab, *lefts]
    aliases = {}
    if out is not None:
        in_specs += [pl.BlockSpec(memory_space=pl.ANY)]
        aliases = {len(operands): 0}
        operands.append(out)
    slots = min(SLOTS, len(lefts) * width // UNIT)
    return pl.pallas_call(
        gram_kernel,
        in_specs=in_specs,
        out_specs=pl.BlockSpec(memory_space=pl.ANY),
        out_shape=jax.ShapeDtypeStruct((rows, cols), jnp.float32),
        scratch_shapes=[pltpu.VMEM((slots, UNIT, cols), jnp.float32), pltpu.SemaphoreType.DMA((slots,))],
        input_output_aliases=aliases,
        compiler_params=pltpu.CompilerParams(vmem_limit_bytes=max(20 << 20, (14 << 20) + 2 * depth * (len(lefts) * width + cols))),
        cost_estimate=pl.CostEstimate(
            flops=2 * len(lefts) * depth * width * cols,
            bytes_accessed=4 * len(lefts) * width * cols,
            transcendentals=0,
        ),
        name="gram_rows",
    )(*operands)


def chunk_widths(width, shares):
    units = width // UNIT
    cuts = [units * sum(shares[:i]) // sum(shares) for i in range(len(shares) + 1)]
    return [UNIT * (cuts[i + 1] - cuts[i]) for i in range(len(shares)) if cuts[i + 1] > cuts[i]]


def tally_kernel(rooms, *refs):
    masks, total_ref, level_ref = refs[:-2], refs[-2], refs[-1]
    tallies = [jnp.sum(ref[...].astype(jnp.float32)) for ref in masks]
    total_ref[0] = sum(tallies)
    fullest = tallies[0] + tallies[-1]
    for j in range(1, len(masks) // 2):
        fullest = jnp.maximum(fullest, tallies[j] + tallies[len(masks) - 1 - j])
    level_ref[0] = sum((fullest > 2.0 * room).astype(jnp.int32) for room in rooms)


def tally(masks, rooms):
    return pl.pallas_call(
        functools.partial(tally_kernel, rooms),
        in_specs=[pl.BlockSpec(memory_space=pltpu.VMEM)] * len(masks),
        out_specs=[pl.BlockSpec(memory_space=pltpu.SMEM)] * 2,
        out_shape=[jax.ShapeDtypeStruct((1,), jnp.float32), jax.ShapeDtypeStruct((1,), jnp.int32)],
        name="tally",
    )(*masks)


def tied(value, *after):
    return lax.optimization_barrier((value, *after))[0]


def exchange(n_dp, n_tp, widths, first_chunk, later, slab_offset, total):
    line = n_tp // 2
    me_dp, me_tp = lax.axis_index("dp"), lax.axis_index("tp")
    me_line, core = me_tp // 2, me_tp % 2
    count = len(widths)
    starts = [sum(widths[:i]) for i in range(count)]
    half = sum(widths)
    rows = 2 * half * line // n_dp

    def swap_dp(value, j):
        return lax.ppermute(value, "dp", [(s, s ^ j) for s in range(n_dp)])

    def swap_core(value):
        return lax.ppermute(value, "tp", [(s, s ^ 1) for s in range(n_tp)])

    def move_line(value, target):
        return lax.ppermute(
            value, "tp", [(2 * s + c, 2 * target(s) + c) for s in range(line) for c in range(2)]
        )

    direct = line // 2 + 1 if line == 4 else line

    def spread(own):
        return [own] + [move_line(own, lambda s, k=k: s ^ k) for k in range(1, direct)]

    def gather_slab(here):
        return [here] + [swap_dp(here, j) for j in range(1, n_dp)]

    def grams(i, sides, mine, other, out):
        lefts = [(mine, other)[side] for side in sides]
        places = [(core, 1 - core)[side] * half + starts[i] for side in sides]
        return gram_rows(lefts, places, slab, total, out, rows)

    which = (me_line ^ me_dp).astype(jnp.int32).reshape(1)
    near = {0: spread(first_chunk)}
    chunks = later()
    slabs = [
        lax.dynamic_slice_in_dim(
            jnp.concatenate([first_chunk] + [chunks[c] for c in range(1, count)], axis=1),
            slab_offset[me_tp], SLAB_DEV, 1,
        )
    ]
    held, crossed = {}, {}
    out, slab = None, None
    for slot in range(1, count + 3):
        near, held, crossed, chunks, slabs, slab, out = lax.optimization_barrier(
            (near, held, crossed, chunks, slabs, slab, out)
        )
        done, after = {}, {}
        i = slot - 1
        if i < count:
            after[i] = near.pop(i)
            if direct < line:
                relay = jnp.where((me_line == 0) | (me_line == 3), after[i][1], after[i][2])
                after[i] = after[i] + [move_line(relay, lambda s: (2, 0, 3, 1)[s])]
        if slot < count:
            near[slot] = spread(chunks[slot])
        if slot == 1:
            slabs = gather_slab(slabs[0])
        if slot == 2:
            slab = joined(slabs)
            slabs = None
        i = slot - 2
        if 0 <= i < count:
            picked = dealt(which, held.pop(i))
            done[i] = [picked[0]] + [swap_dp(picked[j], j) for j in range(1, n_dp)]
        i = slot - 3
        if 0 <= i < count:
            mine = joined(crossed.pop(i))
            other = swap_core(mine)
            if i + 1 < count:
                out = grams(i, (0, 1), mine, other, out)
            else:
                out = grams(i, (0,), mine, other, out)
                out = grams(i, (1,), mine, other, out)
        held.update(after)
        crossed.update(done)
    return out


def mirrored(n_dp, value):
    return lax.ppermute(value, "dp", [(s, n_dp - 1 - s) for s in range(n_dp)])


def share_rows(n_dp, n_tp, room, widths, owns, spares, first, slab_offset, total):
    kept = room - spares[0].shape[0]

    def merged(own, extra):
        return own + jnp.pad(extra, ((kept, 0), (0, 0)))

    def later():
        rest = mirrored(n_dp, spares[1])
        starts = [sum(widths[1:i]) for i in range(1, len(widths) + 1)]
        return {c: merged(owns[c], rest[:, starts[c - 1] : starts[c]]) for c in range(1, len(widths))}

    return exchange(n_dp, n_tp, widths, merged(owns[0], first), later, slab_offset, total)


def all_rows(n_dp, n_tp, widths, owns, spares, slab_offset, total):
    keys = jnp.concatenate(
        [jnp.concatenate(owns, axis=1), jnp.concatenate(spares, axis=1)], axis=0
    )
    starts = [sum(widths[:i]) for i in range(len(widths) + 1)]
    chunks = {c: keys[:, starts[c] : starts[c + 1]] for c in range(len(widths))}
    return exchange(n_dp, n_tp, widths, chunks.pop(0), lambda: chunks, slab_offset, total)


def on_device(n_dp, n_tp, gate_pre, up_pre, token_live, slab_offset):
    tokens, half = gate_pre.shape
    rooms = (tokens * 5 // 8, tokens * 11 // 16)
    widths = chunk_widths(half, SHARES)
    live = token_live[None, :]
    masks = [live] + [lax.ppermute(live, "dp", [(s, s ^ j) for s in range(n_dp)]) for j in range(1, n_dp)]
    owns, spares = live_keys(gate_pre, up_pre, live, rooms[0], widths)
    first = mirrored(n_dp, tied(spares[0], *masks[1:]))
    total, level = tally(masks, rooms)

    def tight(owns, spares, first, gate_pre, up_pre, live, slab_offset, total):
        return share_rows(n_dp, n_tp, rooms[0], widths, owns, spares, first, slab_offset, total)

    def loose(owns, spares, first, gate_pre, up_pre, live, slab_offset, total):
        owns, spares = live_keys(gate_pre, up_pre, live, rooms[1], widths)
        first = mirrored(n_dp, spares[0])
        return share_rows(n_dp, n_tp, rooms[1], widths, owns, spares, first, slab_offset, total)

    def full(owns, spares, first, gate_pre, up_pre, live, slab_offset, total):
        return all_rows(n_dp, n_tp, chunk_widths(half, FULL_SHARES), owns, spares, slab_offset, total)

    return lax.switch(
        level[0], (tight, loose, full), owns, spares, first, gate_pre, up_pre, live, slab_offset, total
    )


def solution(mesh):
    placed = (P("dp", "tp"), P("dp", "tp"), P("dp"), P())
    return jax.shard_map(
        functools.partial(on_device, mesh.shape["dp"], mesh.shape["tp"]),
        mesh=mesh,
        in_specs=placed,
        out_specs=P("dp", "tp"),
        check_vma=False,
    )
```

```python
import functools

import jax
import jax.numpy as jnp
from jax import lax
from jax.experimental import pallas as pl
from jax.experimental.pallas import tpu as pltpu
from jax.sharding import PartitionSpec as P

SLAB_DEV = 1536
UNIT = 256
SLOTS = 4
SHARES = (4, 4, 4, 2)
FULL_SHARES = (7, 7)


def keys_kernel(room, widths, live_ref, gate_ref, up_ref, *refs):
    own_refs, spare_refs = refs[: len(widths)], refs[len(widths) :]
    tokens = gate_ref.shape[0]
    live = live_ref[...].astype(jnp.float32)
    slot_id = lax.broadcasted_iota(jnp.int32, (tokens, tokens), 0)
    token_id = lax.broadcasted_iota(jnp.int32, (tokens, tokens), 1)
    upto = (slot_id <= token_id).astype(jnp.float32)
    rank = (jnp.dot(jnp.broadcast_to(live, (8, tokens)), upto, preferred_element_type=jnp.float32) - 1.0)[:1]
    slot = jnp.where(rank < room, rank, tokens - jnp.sum(live) + rank)
    order = ((slot_id.astype(jnp.float32) == slot) & (live > 0)).astype(jnp.bfloat16)

    def place(columns):
        gate = gate_ref[:, columns].astype(jnp.float32)
        key = (0.5 * gate) * (1.0 + jnp.tanh(0.5 * gate)) * up_ref[:, columns].astype(jnp.float32)
        return jnp.dot(order, key.astype(jnp.bfloat16), preferred_element_type=jnp.float32).astype(jnp.bfloat16)

    for c, width in enumerate(widths):
        start = sum(widths[:c])
        shift = start - widths[0] if c else 0

        def fill(i, carry, c=c, start=start, shift=shift):
            at = pl.multiple_of(i * UNIT, UNIT)
            placed = place(pl.ds(start + at, UNIT))
            own_refs[c][:, pl.ds(at, UNIT)] = placed[:room]
            spare_refs[min(c, 1)][:, pl.ds(shift + at, UNIT)] = placed[room:]
            return carry

        lax.fori_loop(0, width // UNIT, fill, 0)


def live_keys(gate_pre, up_pre, token_live, room, widths):
    tokens, width = gate_pre.shape
    spare = tokens - room
    shapes = [(room, part) for part in widths] + [(spare, widths[0]), (spare, width - widths[0])]
    outs = pl.pallas_call(
        functools.partial(keys_kernel, room, widths),
        in_specs=[pl.BlockSpec(memory_space=pltpu.VMEM)] * 3,
        out_specs=[pl.BlockSpec(memory_space=pltpu.VMEM)] * len(shapes),
        out_shape=[jax.ShapeDtypeStruct(shape, jnp.bfloat16) for shape in shapes],
        compiler_params=pltpu.CompilerParams(vmem_limit_bytes=12 << 20),
        cost_estimate=pl.CostEstimate(
            flops=2 * tokens * tokens * width,
            bytes_accessed=6 * tokens * width,
            transcendentals=tokens * width,
        ),
        name="live_keys",
    )(token_live, gate_pre, up_pre)
    return outs[: len(widths)], outs[len(widths) :]


def join_kernel(*refs):
    parts, out_ref = refs[:-1], refs[-1]
    rows = parts[0].shape[0]
    for i, part in enumerate(parts):
        out_ref[i * rows : (i + 1) * rows, :] = part[...]


def joined(parts):
    rows, cols = parts[0].shape
    return pl.pallas_call(
        join_kernel,
        in_specs=[pl.BlockSpec(memory_space=pltpu.VMEM)] * len(parts),
        out_specs=pl.BlockSpec(memory_space=pltpu.VMEM),
        out_shape=jax.ShapeDtypeStruct((len(parts) * rows, cols), parts[0].dtype),
        compiler_params=pltpu.CompilerParams(vmem_limit_bytes=max(8 << 20, 10 * len(parts) * rows * cols)),
        cost_estimate=pl.CostEstimate(flops=0, bytes_accessed=1 << 20, transcendentals=0),
        name="joined",
    )(*parts)


def deal_kernel(which_ref, *refs):
    count = len(refs) // 2
    for which in range(count):

        @pl.when(which_ref[0] == which)
        def _(which=which):
            for j in range(count):
                refs[count + j][...] = refs[j ^ which][...]


def dealt(which, values):
    return pl.pallas_call(
        deal_kernel,
        in_specs=[pl.BlockSpec(memory_space=pltpu.SMEM)] + [pl.BlockSpec(memory_space=pltpu.VMEM)] * len(values),
        out_specs=[pl.BlockSpec(memory_space=pltpu.VMEM)] * len(values),
        out_shape=[jax.ShapeDtypeStruct(value.shape, value.dtype) for value in values],
        compiler_params=pltpu.CompilerParams(
            vmem_limit_bytes=max(8 << 20, 10 * len(values) * values[0].size)
        ),
        cost_estimate=pl.CostEstimate(flops=0, bytes_accessed=1 << 20, transcendentals=0),
        name="dealt",
    )(which, *values)


def gram_kernel(rows_ref, total_ref, *refs):
    out_ref, held, sent = refs[-3:]
    slab_ref = refs[0]
    lefts = refs[1 : 1 + rows_ref.shape[0]]
    slots = held.shape[0]
    tiles = lefts[0].shape[1] // UNIT
    inv = 1.0 / jnp.full((1, held.shape[2]), total_ref[0], jnp.float32)

    def leave(row, slot):
        row = pl.multiple_of(row, UNIT)
        return pltpu.make_async_copy(held.at[slot], out_ref.at[pl.ds(row, UNIT)], sent.at[slot])

    for side, left_ref in enumerate(lefts):

        def tile(i, carry, side=side, left_ref=left_ref):
            slot = lax.rem(i + side * tiles, slots)

            @pl.when(i + side * tiles >= slots)
            def _():
                leave(0, slot).wait()

            left = left_ref[:, pl.ds(pl.multiple_of(i * UNIT, UNIT), UNIT)]
            gram = lax.dot_general(
                left, slab_ref[...], (((0,), (0,)), ((), ())), preferred_element_type=jnp.float32
            )
            held[slot] = gram * inv
            leave(rows_ref[side] + i * UNIT, slot).start()
            return carry

        lax.fori_loop(0, tiles, tile, 0)
    for slot in range(slots):
        leave(0, slot).wait()


def gram_rows(lefts, starts, slab, total, out, rows):
    depth, width = lefts[0].shape
    cols = slab.shape[1]
    in_specs = [pl.BlockSpec(memory_space=pltpu.SMEM)] * 2
    in_specs += [pl.BlockSpec(memory_space=pltpu.VMEM)] * (1 + len(lefts))
    operands = [jnp.stack(starts), total, slab, *lefts]
    aliases = {}
    if out is not None:
        in_specs += [pl.BlockSpec(memory_space=pl.ANY)]
        aliases = {len(operands): 0}
        operands.append(out)
    slots = min(SLOTS, len(lefts) * width // UNIT)
    return pl.pallas_call(
        gram_kernel,
        in_specs=in_specs,
        out_specs=pl.BlockSpec(memory_space=pl.ANY),
        out_shape=jax.ShapeDtypeStruct((rows, cols), jnp.float32),
        scratch_shapes=[pltpu.VMEM((slots, UNIT, cols), jnp.float32), pltpu.SemaphoreType.DMA((slots,))],
        input_output_aliases=aliases,
        compiler_params=pltpu.CompilerParams(vmem_limit_bytes=max(20 << 20, (14 << 20) + 2 * depth * (len(lefts) * width + cols))),
        cost_estimate=pl.CostEstimate(
            flops=2 * len(lefts) * depth * width * cols,
            bytes_accessed=4 * len(lefts) * width * cols,
            transcendentals=0,
        ),
        name="gram_rows",
    )(*operands)


def chunk_widths(width, shares):
    units = width // UNIT
    cuts = [units * sum(shares[:i]) // sum(shares) for i in range(len(shares) + 1)]
    return [UNIT * (cuts[i + 1] - cuts[i]) for i in range(len(shares)) if cuts[i + 1] > cuts[i]]


def tally_kernel(rooms, *refs):
    masks, total_ref, level_ref = refs[:-2], refs[-2], refs[-1]
    tallies = [jnp.sum(ref[...].astype(jnp.float32)) for ref in masks]
    total_ref[0] = sum(tallies)
    fullest = tallies[0] + tallies[-1]
    for j in range(1, len(masks) // 2):
        fullest = jnp.maximum(fullest, tallies[j] + tallies[len(masks) - 1 - j])
    level_ref[0] = sum((fullest > 2.0 * room).astype(jnp.int32) for room in rooms)


def tally(masks, rooms):
    return pl.pallas_call(
        functools.partial(tally_kernel, rooms),
        in_specs=[pl.BlockSpec(memory_space=pltpu.VMEM)] * len(masks),
        out_specs=[pl.BlockSpec(memory_space=pltpu.SMEM)] * 2,
        out_shape=[jax.ShapeDtypeStruct((1,), jnp.float32), jax.ShapeDtypeStruct((1,), jnp.int32)],
        name="tally",
    )(*masks)


def tied(value, *after):
    return lax.optimization_barrier((value, *after))[0]


def exchange(n_dp, n_tp, widths, first_chunk, later, slab_offset, total):
    line = n_tp // 2
    me_dp, me_tp = lax.axis_index("dp"), lax.axis_index("tp")
    me_line, core = me_tp // 2, me_tp % 2
    count = len(widths)
    starts = [sum(widths[:i]) for i in range(count)]
    half = sum(widths)
    rows = 2 * half * line // n_dp

    def swap_dp(value, j):
        return lax.ppermute(value, "dp", [(s, s ^ j) for s in range(n_dp)])

    def swap_core(value):
        return lax.ppermute(value, "tp", [(s, s ^ 1) for s in range(n_tp)])

    def move_line(value, target):
        return lax.ppermute(
            value, "tp", [(2 * s + c, 2 * target(s) + c) for s in range(line) for c in range(2)]
        )

    direct = line // 2 + 1 if line == 4 else line

    def spread(own):
        return [own] + [move_line(own, lambda s, k=k: s ^ k) for k in range(1, direct)]

    def gather_slab(here):
        return [here] + [swap_dp(here, j) for j in range(1, n_dp)]

    def grams(i, sides, mine, other, out):
        lefts = [(mine, other)[side] for side in sides]
        places = [(core, 1 - core)[side] * half + starts[i] for side in sides]
        return gram_rows(lefts, places, slab, total, out, rows)

    which = (me_line ^ me_dp).astype(jnp.int32).reshape(1)
    near = {0: spread(first_chunk)}
    chunks = later()
    slabs = [
        lax.dynamic_slice_in_dim(
            jnp.concatenate([first_chunk] + [chunks[c] for c in range(1, count)], axis=1),
            slab_offset[me_tp], SLAB_DEV, 1,
        )
    ]
    held, crossed = {}, {}
    out, slab = None, None
    for slot in range(1, count + 3):
        near, held, crossed, chunks, slabs, slab, out = lax.optimization_barrier(
            (near, held, crossed, chunks, slabs, slab, out)
        )
        done, after = {}, {}
        i = slot - 1
        if i < count:
            after[i] = near.pop(i)
            if direct < line:
                relay = jnp.where((me_line == 0) | (me_line == 3), after[i][1], after[i][2])
                after[i] = after[i] + [move_line(relay, lambda s: (2, 0, 3, 1)[s])]
        if slot < count:
            near[slot] = spread(chunks[slot])
        if slot == 1:
            slabs = gather_slab(slabs[0])
        if slot == 2:
            slab = joined(slabs)
            slabs = None
        i = slot - 2
        if 0 <= i < count:
            picked = dealt(which, held.pop(i))
            done[i] = [picked[0]] + [swap_dp(picked[j], j) for j in range(1, n_dp)]
        i = slot - 3
        if 0 <= i < count:
            mine = joined(crossed.pop(i))
            other = swap_core(mine)
            if i + 1 < count:
                out = grams(i, (0, 1), mine, other, out)
            else:
                out = grams(i, (0,), mine, other, out)
                out = grams(i, (1,), mine, other, out)
        held.update(after)
        crossed.update(done)
    return out


def mirrored(n_dp, value):
    return lax.ppermute(value, "dp", [(s, n_dp - 1 - s) for s in range(n_dp)])


def share_rows(n_dp, n_tp, room, widths, owns, spares, first, slab_offset, total):
    kept = room - spares[0].shape[0]

    def merged(own, extra):
        return own + jnp.pad(extra, ((kept, 0), (0, 0)))

    head = merged(owns[0], first)

    def later():
        rest = mirrored(n_dp, tied(spares[1], head))
        starts = [sum(widths[1:i]) for i in range(1, len(widths) + 1)]
        return {c: merged(owns[c], rest[:, starts[c - 1] : starts[c]]) for c in range(1, len(widths))}

    return exchange(n_dp, n_tp, widths, head, later, slab_offset, total)


def all_rows(n_dp, n_tp, widths, owns, spares, slab_offset, total):
    keys = jnp.concatenate(
        [jnp.concatenate(owns, axis=1), jnp.concatenate(spares, axis=1)], axis=0
    )
    starts = [sum(widths[:i]) for i in range(len(widths) + 1)]
    chunks = {c: keys[:, starts[c] : starts[c + 1]] for c in range(len(widths))}
    return exchange(n_dp, n_tp, widths, chunks.pop(0), lambda: chunks, slab_offset, total)


def on_device(n_dp, n_tp, gate_pre, up_pre, token_live, slab_offset):
    tokens, half = gate_pre.shape
    rooms = (tokens * 5 // 8, tokens * 11 // 16)
    widths = chunk_widths(half, SHARES)
    live = token_live[None, :]
    masks = [live] + [lax.ppermute(live, "dp", [(s, s ^ j) for s in range(n_dp)]) for j in range(1, n_dp)]
    owns, spares = live_keys(gate_pre, up_pre, live, rooms[0], widths)
    first = mirrored(n_dp, tied(spares[0], *masks[1:]))
    total, level = tally(masks, rooms)

    def tight(owns, spares, first, gate_pre, up_pre, live, slab_offset, total):
        return share_rows(n_dp, n_tp, rooms[0], widths, owns, spares, first, slab_offset, total)

    def loose(owns, spares, first, gate_pre, up_pre, live, slab_offset, total):
        owns, spares = live_keys(gate_pre, up_pre, live, rooms[1], widths)
        first = mirrored(n_dp, spares[0])
        return share_rows(n_dp, n_tp, rooms[1], widths, owns, spares, first, slab_offset, total)

    def full(owns, spares, first, gate_pre, up_pre, live, slab_offset, total):
        return all_rows(n_dp, n_tp, chunk_widths(half, FULL_SHARES), owns, spares, slab_offset, total)

    return lax.switch(
        level[0], (tight, loose, full), owns, spares, first, gate_pre, up_pre, live, slab_offset, total
    )


def solution(mesh):
    placed = (P("dp", "tp"), P("dp", "tp"), P("dp"), P())
    return jax.shard_map(
        functools.partial(on_device, mesh.shape["dp"], mesh.shape["tp"]),
        mesh=mesh,
        in_specs=placed,
        out_specs=P("dp", "tp"),
        check_vma=False,
    )
```
